256 devices in a mesh: rep: 32 (over z_lo, x, core), fsdp: 8 (over y, z_hi).
Axes of the slice: x: 4, y: 4, z: 8 (z_hi: 2, z_lo: 4; z = z_hi * 4 + z_lo), core: 2. Of those that a mesh axis runs over, the one named last changes fastest.
Arguments:
- global_weights: bfloat16 [8192, 1024], P(None, 'fsdp'), may hold values from -0.75 to 0.75
- momentum: float32 [8192, 1024], P('rep', 'fsdp'), may hold values from -0.3125 to 0.3125
- first_moment: float32 [32, 8192, 1024], P('rep', None, 'fsdp'), may hold values from -0.0029296875 to 0.0029296875
- second_moment: float32 [32, 8192, 1024], P('rep', None, 'fsdp'), may hold values from 1e-08 to 1e-07
- hidden_bank: bfloat16 [32, 256, 8192], P('rep', 'fsdp'), may hold values from -0.15625 to 0.15625
- target_bank: bfloat16 [32, 256, 1024], P('rep', None, 'fsdp'), may hold values from -6 to 6
- token_ids: int32 [32, 2, 512], P('rep'), may hold values from 0 to 255
Outputs:
- new_weights: bfloat16 [8192, 1024], P(None, 'fsdp')
- new_momentum: float32 [8192, 1024], P('rep', 'fsdp')
The draws below stay inside these ranges and needn't reach their ends.
All inputs are finite; a program needn't handle non-finite values.
Results may differ from the reference program's by a relative error of at most 0.0034.
Values may be sent and summed in bfloat16 or wider, within the bound.
A program may use at most 128 MiB of HBM per device.

```python
import math
import jax
import jax.numpy as jnp
from jax import lax

D = 8192
KVW = 1024
TOK = 512
INNER = 2
STORE = 256
REPLICAS = 32


def with_ends(array, key, low, high):
    place = [jax.random.randint(jax.random.fold_in(key, axis), (), 0, length) for axis, length in enumerate(array.shape)]
    main_axis = array.shape.index(max(array.shape))
    beside = place[:main_axis] + [(place[main_axis] + 1) % array.shape[main_axis]] + place[main_axis + 1:]
    return array.at[tuple(place)].set(low).at[tuple(beside)].set(high)


def levels(own_key, shape, cuts, least, largest):
    def one(dim, shards_of):
        heights = jax.random.uniform(jax.random.fold_in(jax.random.fold_in(own_key, 6), dim), (shards_of,), jnp.float32, least / len(cuts), largest / len(cuts))
        return jnp.repeat(jnp.exp(heights), shape[dim] // shards_of).reshape((-1,) + (1,) * (len(shape) - dim - 1))

    factor_of = one(*cuts[0])
    for cut in cuts[1:]:
        factor_of = factor_of * one(*cut)
    return factor_of


def bell_draw(own_key, dims, deviation, bound, cuts=(), held_as=jnp.bfloat16):
    array = deviation * jax.random.normal(own_key, dims, jnp.float32)
    if cuts:
        array = array * levels(own_key, dims, cuts, -0.22, 0.18)
    return jnp.clip(array, -bound, bound).astype(held_as)


def setup_inputs(seed: int = 0) -> dict:
    key_list = jax.random.split(jax.random.key(seed), 8)
    global_weights = bell_draw(key_list[0], (D, KVW), 0.05, 0.75, ((1, 8),))
    momentum = bell_draw(key_list[1], (D, KVW), 0.02, 0.3125, ((0, 32), (1, 8)), jnp.float32)
    first_moment = bell_draw(key_list[2], (REPLICAS, D, KVW), 0.0002, 0.0029296875, ((0, 32), (2, 8)), jnp.float32)
    second_moment = jnp.clip(jnp.exp(math.log(1.0000000116860974e-07) - 2.3025851 * jax.random.uniform(key_list[3], (REPLICAS, D, KVW), jnp.float32) ** levels(key_list[3], (REPLICAS, D, KVW), ((0, 32), (2, 8)), -0.2, 0.2)), 9.99999993922529e-09, 1.0000000116860974e-07)
    hidden_bank = bell_draw(key_list[4], (REPLICAS, STORE, D), (D ** -0.5), 0.15625, ((0, 32), (1, 8)))
    target_bank = bell_draw(key_list[5], (REPLICAS, STORE, KVW), 1.0, 6.0, ((0, 32), (2, 8)))
    token_ids = with_ends(jax.random.randint(key_list[6], (REPLICAS, INNER, TOK), 0, STORE), jax.random.fold_in(key_list[6], 1), 0, STORE - 1).astype(jnp.int32)
    return {"global_weights": global_weights, "momentum": momentum, "first_moment": first_moment, "second_moment": second_moment, "hidden_bank": hidden_bank, "target_bank": target_bank, "token_ids": token_ids}


def reference(global_weights, momentum, first_moment, second_moment, hidden_bank, target_bank, token_ids):
    start = global_weights.astype(jnp.float32)

    def replica(total, members):
        first_state, second_state, bank_rows, targets, ids_all = members
        weights = start
        for inner_step in range(INNER):
            chosen = ids_all[inner_step].astype(jnp.int32)
            picked = jnp.take(bank_rows, chosen, axis=0)
            wanted = jnp.take(targets, chosen, axis=0)
            output = jnp.dot(picked, weights.astype(jnp.bfloat16), preferred_element_type=jnp.float32)
            residual_out = ((output - wanted.astype(jnp.float32)) / TOK).astype(jnp.bfloat16)
            gradient = jnp.dot(picked.T, residual_out, preferred_element_type=jnp.float32)
            first_state = 0.9 * first_state + 0.1 * gradient
            second_state = 0.95 * second_state + 0.05 * gradient * gradient
            weights = weights - 0.1 * (first_state / (jnp.sqrt(second_state) + 1e-08) + 0.1 * weights)
        return (total + (start - weights), None)
    summed, unused = lax.scan(replica, jnp.zeros_like(start), (first_moment, second_moment, hidden_bank, target_bank, token_ids))
    average = summed / REPLICAS
    new_momentum = 0.9 * momentum + average
    new_weights = (start - 0.7 * (average + 0.9 * new_momentum)).astype(jnp.bfloat16)
    return (new_weights, new_momentum)
```

```python
import jax
import jax.numpy as jnp
from jax import lax
from jax.sharding import PartitionSpec as P


def per_device(
    global_weights, momentum, first_moment, second_moment, hidden_bank, target_bank, token_ids
):
    ids_all = token_ids[0]
    inner_count, token_count = ids_all.shape
    bank = lax.all_gather(hidden_bank[0], "fsdp", axis=0, tiled=True)
    store = bank.shape[0]
    targets = target_bank[0].astype(jnp.float32)
    counts = (ids_all[:, None, :] == jnp.arange(store, dtype=jnp.int32)[None, :, None]).astype(
        jnp.float32
    ).sum(axis=2)
    start_weights = global_weights.astype(jnp.float32)
    weights = start_weights
    first_state = first_moment[0]
    second_state = second_moment[0]
    for inner_step in range(inner_count):
        output = jnp.dot(bank, weights.astype(jnp.bfloat16), preferred_element_type=jnp.float32)
        residual = ((output - targets) / token_count).astype(jnp.bfloat16).astype(jnp.float32)
        scaled = (residual * counts[inner_step][:, None]).astype(jnp.bfloat16)
        gradient = lax.dot_general(
            bank, scaled, (((0,), (0,)), ((), ())), preferred_element_type=jnp.float32
        )
        first_state = 0.9 * first_state + 0.1 * gradient
        second_state = 0.95 * second_state + 0.05 * gradient * gradient
        weights = weights - 0.1 * (first_state / (jnp.sqrt(second_state) + 1e-08) + 0.1 * weights)
    local_change = start_weights - weights
    share_rows = momentum.shape[0]
    row_begin = lax.axis_index("rep") * share_rows
    summed = lax.psum_scatter(local_change, "rep", scatter_dimension=0, tiled=True)
    average = summed / lax.axis_size("rep")
    new_momentum = 0.9 * momentum + average
    start_share = lax.dynamic_slice_in_dim(start_weights, row_begin, share_rows, 0)
    new_share = (start_share - 0.7 * (average + 0.9 * new_momentum)).astype(jnp.bfloat16)
    new_weights = lax.all_gather(new_share, "rep", axis=0, tiled=True)
    return (new_weights, new_momentum)


def solution(mesh):
    return jax.shard_map(
        per_device,
        mesh=mesh,
        in_specs=(
            P(None, "fsdp"),
            P("rep", "fsdp"),
            P("rep", None, "fsdp"),
            P("rep", None, "fsdp"),
            P("rep", "fsdp", None),
            P("rep", None, "fsdp"),
            P("rep", None, None),
        ),
        out_specs=(P(None, "fsdp"), P("rep", "fsdp")),
        check_vma=False,
    )
```

```python
import jax
import jax.numpy as jnp
from jax import lax
from jax.experimental import pallas as pl
from jax.experimental.pallas import tpu as pltpu
from jax.sharding import PartitionSpec as P

F32 = jnp.float32
BF16 = jnp.bfloat16
MESH = pl.DeviceIdType.MESH

Z_LO, Z_HI, X, Y, CORES = 4, 2, 4, 4, 2

CHUNKS = 4
STEP_ROWS = 512
ORDER = (2, 1, 3, 0)


def round_kernel(
    weights_hbm, momentum_ref, first_hbm, second_hbm, bank_hbm, target_ref, ids_ref,
    out_weights, out_momentum,
    bank, bank_t, relay, w0, w1, first, second, count, acc, scaled,
    pair_send, pair_recv, own_sum, far_send, far_recv, near_send, near_recv,
    line_send, line_recv, total, gathered,
    send_sems, recv_sems, local_sems,
):
    rep, fsdp = lax.axis_index("rep"), lax.axis_index("fsdp")
    core = rep % CORES
    x = (rep // CORES) % X
    z_lo = rep // (CORES * X)
    z_hi = fsdp % Z_HI
    y = fsdp // Z_HI
    depth = Z_LO * Z_HI
    z = z_hi * Z_LO + z_lo

    def device(x_at, y_at, z_at, core_at):
        return (((z_at % Z_LO) * X + x_at) * CORES + core_at, y_at * Z_HI + z_at // Z_LO)

    def line(distance):
        return z_hi * Z_LO + (z_lo + distance) % Z_LO

    y_up, y_down = device(x, (y + 1) % Y, z, core), device(x, (y + Y - 1) % Y, z, core)
    z_up, z_down = device(x, y, (z + 2) % depth, core), device(x, y, (z + depth - 2) % depth, core)
    x_up, x_down = device((x + 1) % X, y, z, core), device((x + X - 1) % X, y, z, core)
    pair = device(x, y, z, 1 - core)
    line_peers = {d: device(x, y, line(d), core) for d in (1, 2, 3)}

    barrier = pltpu.get_barrier_semaphore()
    peers = [y_up, y_down, z_up, z_down, x_up, x_down, pair] + [line_peers[d] for d in (1, 2, 3)]
    for peer in peers:
        pl.semaphore_signal(barrier, inc=1, device_id=peer, device_id_type=MESH)
    pl.semaphore_wait(barrier, len(peers))

    sent = []
    placed = []

    def send(src, dst, peer):
        at = len(sent)
        copy = pltpu.make_async_remote_copy(
            src_ref=src, dst_ref=dst, send_sem=send_sems.at[at], recv_sem=recv_sems.at[at],
            device_id=peer, device_id_type=MESH,
        )
        copy.start()
        sent.append(copy)
        return copy

    def place(src, dst):
        copy = pltpu.make_async_copy(src, dst, local_sems.at[len(placed)])
        copy.start()
        placed.append(copy)
        return copy

    rows_all, columns_all = bank.shape
    block = bank_hbm.shape[1]
    half = block // 2
    wide = columns_all // CHUNKS

    def part(slot, q, which=None):
        cols = pl.ds(q * wide, wide)
        if which is None:
            return bank.at[pl.ds(slot * block, block), cols]
        return bank.at[pl.ds(slot * block + which * half, half), cols]

    def own_part(q, which=None):
        cols = pl.ds(q * wide, wide)
        if which is None:
            return bank_hbm.at[0, :, cols]
        return bank_hbm.at[0, pl.ds(which * half, half), cols]

    def relay_part(q, which):
        return relay.at[which, :, pl.ds(q * wide, wide)]

    def z_first(q):
        return (send(own_part(q, 0), relay_part(q, 0), z_up),
                send(own_part(q, 1), relay_part(q, 1), z_down))

    z_own = {0: z_first(0)}
    y_own = {}
    for q in range(CHUNKS):
        y_own[q] = (send(own_part(q), part(1, q), y_up), send(own_part(q), part(2, q), y_down))
        if q == 0:
            z_own[1] = z_first(1)
    own_here = place(bank_hbm.at[0], bank.at[pl.ds(0, block), :])
    states_here = [
        place(weights_hbm, w0), place(first_hbm.at[0], first), place(second_hbm.at[0], second)
    ]

    inner_count, token_count = ids_ref.shape[1], ids_ref.shape[2]
    starts = []
    for z_of in (z_hi, 1 - z_hi):
        for y_of in (y, (y + Y - 1) % Y, (y + 1) % Y, (y + 2) % Y):
            starts.append(pl.multiple_of((y_of * Z_HI + z_of) * block, block))
    for k in range(inner_count):
        ids = jnp.broadcast_to(ids_ref[0, k:k + 1, :], (block, token_count))
        for slot, start in enumerate(starts):
            row = lax.broadcasted_iota(jnp.int32, (block, token_count), 0) + start
            hits = jnp.where(ids == row, 1.0, 0.0).astype(F32)
            number = jnp.sum(hits, axis=1, keepdims=True)
            count[k, pl.ds(slot * block, block), :] = jnp.broadcast_to(number, (block, 128))

    z_relayed, y_passed, y_partner, partner_passed = {}, {}, {}, {}
    for q in range(CHUNKS):
        for copy in z_own[q]:
            copy.wait_recv()
        z_relayed[q] = (send(relay_part(q, 0), part(4, q, 0), z_up),
                        send(relay_part(q, 1), part(4, q, 1), z_down))
        if q + 2 < CHUNKS:
            z_own[q + 2] = z_first(q + 2)
        for copy in y_own[q]:
            copy.wait_recv()
        y_passed[q] = (send(part(1, q, 0), part(3, q, 0), y_up),
                       send(part(2, q, 1), part(3, q, 1), y_down))

    def partner_on(q):
        for copy in z_relayed[q]:
            copy.wait_recv()
        y_partner[q] = (send(part(4, q), part(5, q), y_up), send(part(4, q), part(6, q), y_down))

    def partner_pass(q):
        for copy in y_partner[q]:
            copy.wait_recv()
        partner_passed[q] = (send(part(5, q, 0), part(7, q, 0), y_up),
                             send(part(6, q, 1), part(7, q, 1), y_down))

    group = rows_all // 2

    def first_product(g, q):
        rows = pl.ds(g * group, group)

        def body(i, unused):
            cols = pl.ds(pl.multiple_of(q * wide + i * 512, 512), 512)
            tile = bank[rows, cols]
            acc[rows, :] += jnp.dot(tile, w0[cols, :], preferred_element_type=F32)
            bank_t[cols, rows] = tile.T
            return unused

        lax.fori_loop(0, wide // 512, body, 0)

    acc[...] = jnp.zeros_like(acc)
    partner_on(0)
    partner_on(1)
    own_here.wait()
    for copy in states_here:
        copy.wait()
    for q in range(CHUNKS):
        for copy in y_passed[q]:
            copy.wait_recv()
        first_product(0, q)
        if q + 2 < CHUNKS:
            partner_on(q + 2)
        else:
            partner_pass(q + 2 - CHUNKS)
    for q in range(2, CHUNKS):
        partner_pass(q)
    for q in range(CHUNKS):
        for copy in partner_passed[q]:
            copy.wait_recv()
        first_product(1, q)

    def weigh(k):
        for slot, start in enumerate(starts):
            rows = pl.ds(slot * block, block)
            wanted = target_ref[0, pl.ds(start, block), :].astype(F32)
            residual = ((acc[rows, :] - wanted) / token_count).astype(BF16).astype(F32)
            scaled[rows, :] = (residual * count[k, rows, :]).astype(BF16)

    def moments(rows):
        gradient = jnp.dot(bank_t[rows, :], scaled[...], preferred_element_type=F32)
        m = 0.9 * first[rows, :] + 0.1 * gradient
        v = 0.95 * second[rows, :] + 0.05 * gradient * gradient
        return m, v

    def stepped(w, m, v):
        return w - 0.1 * (m / (jnp.sqrt(v) + 1e-08) + 0.1 * w)

    weigh(0)
    acc[...] = jnp.zeros_like(acc)

    def first_step(i, unused):
        rows = pl.ds(pl.multiple_of(i * STEP_ROWS, STEP_ROWS), STEP_ROWS)
        m, v = moments(rows)
        first[rows, :] = m
        second[rows, :] = v
        w = stepped(w0[rows, :].astype(F32), m, v)
        w1[rows, :] = w
        acc[...] += jnp.dot(bank[:, rows], w.astype(BF16), preferred_element_type=F32)
        return unused

    lax.fori_loop(0, columns_all // STEP_ROWS, first_step, 0)
    weigh(1)

    share = momentum_ref.shape[0]

    def change(x_dist, z_dist, core_at):
        row_block = (((z_lo + z_dist) % Z_LO) * X + (x + x_dist) % X) * CORES + core_at
        rows = pl.ds(pl.multiple_of(row_block * share, share), share)
        m, v = moments(rows)
        return w0[rows, :].astype(F32) - stepped(w1[rows, :], m, v)

    pair_copies = {}

    def for_pair(x_dist):
        def body(z_dist, unused):
            pair_send[x_dist, z_dist] = change(x_dist, z_dist, 1 - core).astype(BF16)
            return unused

        lax.fori_loop(0, Z_LO, body, 0)
        pair_copies[x_dist] = send(pair_send.at[x_dist], pair_recv.at[x_dist], pair)

    def for_own(x_dist):
        pair_copies[x_dist].wait_recv()

        def body(z_dist, unused):
            both = change(x_dist, z_dist, core) + pair_recv[x_dist, z_dist].astype(F32)
            if x_dist == 2:
                far_send[z_dist] = both.astype(BF16)
            else:
                own_sum[x_dist, z_dist] = both
            return unused

        lax.fori_loop(0, Z_LO, body, 0)

    mid = share // 2
    low, high = pl.ds(0, mid), pl.ds(mid, mid)
    far_copies, near_up, near_down = {}, {}, {}

    def pass_up(z_dist):
        far_copies[z_dist][0].wait_recv()
        near_send[0, z_dist, low, :] = (
            own_sum[1, z_dist, low, :] + far_recv[0, z_dist].astype(F32)
        ).astype(BF16)
        near_send[0, z_dist, high, :] = own_sum[1, z_dist, high, :].astype(BF16)
        near_up[z_dist] = send(near_send.at[0, z_dist], near_recv.at[0, z_dist], x_up)

    def pass_down(z_dist):
        far_copies[z_dist][1].wait_recv()
        near_send[1, z_dist, high, :] = (
            own_sum[3, z_dist, high, :] + far_recv[1, z_dist].astype(F32)
        ).astype(BF16)
        near_send[1, z_dist, low, :] = own_sum[3, z_dist, low, :].astype(BF16)
        near_down[z_dist] = send(near_send.at[1, z_dist], near_recv.at[1, z_dist], x_down)

    for_pair(2)
    for_pair(1)
    for_own(2)
    for d in ORDER:
        far_copies[d] = (send(far_send.at[d, low], far_recv.at[0, d], x_up),
                         send(far_send.at[d, high], far_recv.at[1, d], x_down))
    for_pair(3)
    for_own(1)
    for_pair(0)
    for_own(3)
    for d in ORDER:
        pass_up(d)
        pass_down(d)
    for_own(0)

    line_copies = {}
    for d in ORDER:
        near_up[d].wait_recv()
        near_down[d].wait_recv()
        summed = (
            own_sum[0, d] + near_recv[0, d].astype(F32) + near_recv[1, d].astype(F32)
        )
        if d:
            line_send[d - 1] = summed.astype(BF16)
            line_copies[d] = send(line_send.at[d - 1], line_recv.at[d - 1], line_peers[d])
        else:
            total[...] = summed
    for d in (1, 3, 2):
        line_copies[d].wait_recv()
    average = (
        total[...] + line_recv[0].astype(F32) + line_recv[1].astype(F32) + line_recv[2].astype(F32)
    ) / (Z_LO * X * CORES)
    new_momentum = 0.9 * momentum_ref[...] + average
    out_momentum[...] = new_momentum
    own_rows = pl.ds(pl.multiple_of(rep * share, share), share)
    start_share = w0[own_rows, :].astype(F32)
    gathered[z_lo, x] = (start_share - 0.7 * (average + 0.9 * new_momentum)).astype(BF16)

    pair_got = []

    def z_from(d):
        return (z_lo + Z_LO - d) % Z_LO

    def keep(d, x_dist):
        z_at, x_at = z_from(d), (x + x_dist) % X
        at = ((z_at * X + x_at) * CORES + core) * share
        out = out_weights.at[pl.ds(pl.multiple_of(at, share), share), :]
        here = gathered.at[z_at, x_at]
        place(here, out)
        pair_got.append(send(here, out, pair))

    def round_x(d):
        here = gathered.at[z_from(d), x]
        return send(here, here, x_up), send(here, here, x_down)

    def onward(d):
        up, down = round_copies[d]
        up.wait_recv()
        here = gathered.at[z_from(d), (x + X - 1) % X, low]
        above = send(here, here, x_up)
        down.wait_recv()
        here = gathered.at[z_from(d), (x + 1) % X, high]
        below = send(here, here, x_down)
        keep(d, X - 1)
        keep(d, 1)
        return above, below

    own_block = gathered.at[z_lo, x]
    line_got = {d: send(own_block, own_block, line_peers[d]) for d in (1, 3, 2)}
    round_copies = {0: round_x(0)}
    keep(0, 0)
    onward_copies = {}
    for d in (1, 3, 2):
        line_got[d].wait_recv()
        round_copies[d] = round_x(d)
        keep(d, 0)
        previous = {1: 0, 3: 1, 2: 3}[d]
        onward_copies[previous] = onward(previous)
    onward_copies[2] = onward(2)
    for d in (0, 1, 3, 2):
        for copy in onward_copies[d]:
            copy.wait_recv()
        keep(d, 2)

    for copy in pair_got:
        copy.wait_recv()
    for copy in sent:
        copy.wait_send()
    for copy in placed[4:]:
        copy.wait()


def per_device(
    global_weights, momentum, first_moment, second_moment, hidden_bank, target_bank, token_ids
):
    depth, width = global_weights.shape
    block = hidden_bank.shape[1]
    store = target_bank.shape[1]
    inner_count = token_ids.shape[1]
    share = momentum.shape[0]
    anywhere = pl.BlockSpec(memory_space=pl.ANY)
    inside = pl.BlockSpec(memory_space=pltpu.VMEM)
    vmem = pltpu.VMEM
    return pl.pallas_call(
        round_kernel,
        out_shape=(
            jax.ShapeDtypeStruct((depth, width), BF16),
            jax.ShapeDtypeStruct((share, width), F32),
        ),
        in_specs=[anywhere, inside, anywhere, anywhere, anywhere, inside, inside],
        out_specs=(anywhere, inside),
        scratch_shapes=[
            vmem((store, depth), BF16),
            vmem((depth, store), BF16),
            vmem((2, block // 2, depth), BF16),
            vmem((depth, width), BF16),
            vmem((depth, width), F32),
            vmem((depth, width), F32),
            vmem((depth, width), F32),
            vmem((inner_count, store, width), F32),
            vmem((store, width), F32),
            vmem((store, width), BF16),
            vmem((X, Z_LO, share, width), BF16),
            vmem((X, Z_LO, share, width), BF16),
            vmem((X, Z_LO, share, width), F32),
            vmem((Z_LO, share, width), BF16),
            vmem((2, Z_LO, share // 2, width), BF16),
            vmem((2, Z_LO, share, width), BF16),
            vmem((2, Z_LO, share, width), BF16),
            vmem((Z_LO - 1, share, width), BF16),
            vmem((Z_LO - 1, share, width), BF16),
            vmem((share, width), F32),
            vmem((Z_LO, X, share, width), BF16),
            pltpu.SemaphoreType.DMA((112,)),
            pltpu.SemaphoreType.DMA((112,)),
            pltpu.SemaphoreType.DMA((24,)),
        ],
        compiler_params=pltpu.CompilerParams(
            collective_id=0, has_side_effects=True, vmem_limit_bytes=60 * 1024 * 1024
        ),
        name="diloco_round",
    )(
        global_weights, momentum, first_moment, second_moment, hidden_bank, target_bank, token_ids
    )


def solution(mesh):
    return jax.shard_map(
        per_device,
        mesh=mesh,
        in_specs=(
            P(None, "fsdp"),
            P("rep", "fsdp"),
            P("rep", None, "fsdp"),
            P("rep", None, "fsdp"),
            P("rep", "fsdp", None),
            P("rep", None, "fsdp"),
            P("rep", None, None),
        ),
        out_specs=(P(None, "fsdp"), P("rep", "fsdp")),
        check_vma=False,
    )
```

```python
import jax
import jax.numpy as jnp
from jax import lax
from jax.experimental import pallas as pl
from jax.experimental.pallas import tpu as pltpu
from jax.sharding import PartitionSpec as P

F32 = jnp.float32
BF16 = jnp.bfloat16
MESH = pl.DeviceIdType.MESH

Z_LO, Z_HI, X, Y, CORES = 4, 2, 4, 4, 2

CHUNKS = 4
STEP_ROWS = 512
ORDER = (2, 1, 3, 0)


def round_kernel(
    weights_hbm, momentum_ref, first_hbm, second_hbm, bank_hbm, target_ref, ids_ref,
    out_weights, out_momentum,
    bank, bank_t, relay, w0, w1, first, second, count, acc, scaled,
    pair_send, pair_recv, own_sum, far_send, far_recv, near_send, near_recv,
    line_send, line_recv, total,
    send_sems, recv_sems, local_sems,
):
    rep, fsdp = lax.axis_index("rep"), lax.axis_index("fsdp")
    core = rep % CORES
    x = (rep // CORES) % X
    z_lo = rep // (CORES * X)
    z_hi = fsdp % Z_HI
    y = fsdp // Z_HI
    depth = Z_LO * Z_HI
    z = z_hi * Z_LO + z_lo

    def device(x_at, y_at, z_at, core_at):
        return (((z_at % Z_LO) * X + x_at) * CORES + core_at, y_at * Z_HI + z_at // Z_LO)

    def line(distance):
        return z_hi * Z_LO + (z_lo + distance) % Z_LO

    y_up, y_down = device(x, (y + 1) % Y, z, core), device(x, (y + Y - 1) % Y, z, core)
    z_up, z_down = device(x, y, (z + 2) % depth, core), device(x, y, (z + depth - 2) % depth, core)
    x_up, x_down = device((x + 1) % X, y, z, core), device((x + X - 1) % X, y, z, core)
    pair = device(x, y, z, 1 - core)
    line_peers = {d: device(x, y, line(d), core) for d in (1, 2, 3)}

    barrier = pltpu.get_barrier_semaphore()
    peers = [y_up, y_down, z_up, z_down, x_up, x_down, pair] + [line_peers[d] for d in (1, 2, 3)]
    for peer in peers:
        pl.semaphore_signal(barrier, inc=1, device_id=peer, device_id_type=MESH)
    pl.semaphore_wait(barrier, len(peers))

    sent = []
    placed = []

    def send(src, dst, peer):
        at = len(sent)
        copy = pltpu.make_async_remote_copy(
            src_ref=src, dst_ref=dst, send_sem=send_sems.at[at], recv_sem=recv_sems.at[at],
            device_id=peer, device_id_type=MESH,
        )
        copy.start()
        sent.append(copy)
        return copy

    def place(src, dst):
        copy = pltpu.make_async_copy(src, dst, local_sems.at[len(placed)])
        copy.start()
        placed.append(copy)
        return copy

    rows_all, columns_all = bank.shape
    block = bank_hbm.shape[1]
    half = block // 2
    wide = columns_all // CHUNKS

    def part(slot, q, which=None):
        cols = pl.ds(q * wide, wide)
        if which is None:
            return bank.at[pl.ds(slot * block, block), cols]
        return bank.at[pl.ds(slot * block + which * half, half), cols]

    def own_part(q, which=None):
        cols = pl.ds(q * wide, wide)
        if which is None:
            return bank_hbm.at[0, :, cols]
        return bank_hbm.at[0, pl.ds(which * half, half), cols]

    def relay_part(q, which):
        return relay.at[which, :, pl.ds(q * wide, wide)]

    def z_first(q):
        return (send(own_part(q, 0), relay_part(q, 0), z_up),
                send(own_part(q, 1), relay_part(q, 1), z_down))

    z_own = {0: z_first(0)}
    y_own = {}
    for q in range(CHUNKS):
        y_own[q] = (send(own_part(q), part(1, q), y_up), send(own_part(q), part(2, q), y_down))
        if q == 0:
            z_own[1] = z_first(1)
    own_here = place(bank_hbm.at[0], bank.at[pl.ds(0, block), :])
    states_here = [
        place(weights_hbm, w0), place(first_hbm.at[0], first), place(second_hbm.at[0], second)
    ]

    inner_count, token_count = ids_ref.shape[1], ids_ref.shape[2]
    starts = []
    for z_of in (z_hi, 1 - z_hi):
        for y_of in (y, (y + Y - 1) % Y, (y + 1) % Y, (y + 2) % Y):
            starts.append(pl.multiple_of((y_of * Z_HI + z_of) * block, block))
    for k in range(inner_count):
        ids = jnp.broadcast_to(ids_ref[0, k:k + 1, :], (block, token_count))
        for slot, start in enumerate(starts):
            row = lax.broadcasted_iota(jnp.int32, (block, token_count), 0) + start
            hits = jnp.where(ids == row, 1.0, 0.0).astype(F32)
            number = jnp.sum(hits, axis=1, keepdims=True)
            count[k, pl.ds(slot * block, block), :] = jnp.broadcast_to(number, (block, 128))

    z_relayed, y_passed, y_partner, partner_passed = {}, {}, {}, {}

    def relay_on(q):
        for copy in z_own[q]:
            copy.wait_recv()
        z_relayed[q] = (send(relay_part(q, 0), part(4, q, 0), z_up),
                        send(relay_part(q, 1), part(4, q, 1), z_down))
        if q + 2 < CHUNKS:
            z_own[q + 2] = z_first(q + 2)

    def own_pass(q):
        for copy in y_own[q]:
            copy.wait_recv()
        y_passed[q] = (send(part(1, q, 0), part(3, q, 0), y_up),
                       send(part(2, q, 1), part(3, q, 1), y_down))

    def partner_on(q):
        for copy in z_relayed[q]:
            copy.wait_recv()
        y_partner[q] = (send(part(4, q), part(5, q), y_up), send(part(4, q), part(6, q), y_down))

    def partner_pass(q):
        for copy in y_partner[q]:
            copy.wait_recv()
        partner_passed[q] = (send(part(5, q, 0), part(7, q, 0), y_up),
                             send(part(6, q, 1), part(7, q, 1), y_down))

    group = rows_all // 2

    def product(g, q):
        for copy in (y_passed, partner_passed)[g][q]:
            copy.wait_recv()
        rows = pl.ds(g * group, group)

        def body(i, unused):
            cols = pl.ds(pl.multiple_of(q * wide + i * 512, 512), 512)
            tile = bank[rows, cols]
            acc[rows, :] += jnp.dot(tile, w0[cols, :], preferred_element_type=F32)
            bank_t[cols, rows] = tile.T
            return unused

        lax.fori_loop(0, wide // 512, body, 0)

    acc[...] = jnp.zeros_like(acc)
    relay_on(0)
    own_pass(0)
    own_pass(1)
    relay_on(1)
    own_pass(2)
    partner_on(0)
    own_pass(3)
    relay_on(2)
    own_here.wait()
    for copy in states_here:
        copy.wait()
    product(0, 0)
    partner_on(1)
    product(0, 1)
    relay_on(3)
    partner_pass(0)
    product(0, 2)
    partner_on(2)
    partner_pass(1)
    product(0, 3)
    partner_on(3)
    partner_pass(2)
    product(1, 0)
    partner_pass(3)
    for q in range(1, CHUNKS):
        product(1, q)

    def weigh(k):
        for slot, start in enumerate(starts):
            rows = pl.ds(slot * block, block)
            wanted = target_ref[0, pl.ds(start, block), :].astype(F32)
            residual = ((acc[rows, :] - wanted) / token_count).astype(BF16).astype(F32)
            scaled[rows, :] = (residual * count[k, rows, :]).astype(BF16)

    def moments(rows):
        gradient = jnp.dot(bank_t[rows, :], scaled[...], preferred_element_type=F32)
        m = 0.9 * first[rows, :] + 0.1 * gradient
        v = 0.95 * second[rows, :] + 0.05 * gradient * gradient
        return m, v

    def stepped(w, m, v):
        return w - 0.1 * (m / (jnp.sqrt(v) + 1e-08) + 0.1 * w)

    weigh(0)
    acc[...] = jnp.zeros_like(acc)

    def first_step(i, unused):
        rows = pl.ds(pl.multiple_of(i * STEP_ROWS, STEP_ROWS), STEP_ROWS)
        m, v = moments(rows)
        first[rows, :] = m
        second[rows, :] = v
        w = stepped(w0[rows, :].astype(F32), m, v)
        w1[rows, :] = w
        acc[...] += jnp.dot(bank[:, rows], w.astype(BF16), preferred_element_type=F32)
        return unused

    lax.fori_loop(0, columns_all // STEP_ROWS, first_step, 0)
    weigh(1)

    share = momentum_ref.shape[0]

    def change(x_dist, z_dist, core_at):
        row_block = (((z_lo + z_dist) % Z_LO) * X + (x + x_dist) % X) * CORES + core_at
        rows = pl.ds(pl.multiple_of(row_block * share, share), share)
        m, v = moments(rows)
        return w0[rows, :].astype(F32) - stepped(w1[rows, :], m, v)

    pair_copies = {}

    def for_pair(x_dist):
        def body(z_dist, unused):
            pair_send[x_dist, z_dist] = change(x_dist, z_dist, 1 - core).astype(BF16)
            return unused

        lax.fori_loop(0, Z_LO, body, 0)
        pair_copies[x_dist] = send(pair_send.at[x_dist], pair_recv.at[x_dist], pair)

    def for_own(x_dist):
        pair_copies[x_dist].wait_recv()

        def body(z_dist, unused):
            both = change(x_dist, z_dist, core) + pair_recv[x_dist, z_dist].astype(F32)
            if x_dist == 2:
                far_send[z_dist] = both.astype(BF16)
            else:
                own_sum[x_dist, z_dist] = both
            return unused

        lax.fori_loop(0, Z_LO, body, 0)

    mid = share // 2
    low, high = pl.ds(0, mid), pl.ds(mid, mid)
    far_copies, near_up, near_down = {}, {}, {}

    def pass_up(z_dist):
        far_copies[z_dist][0].wait_recv()
        near_send[0, z_dist, low, :] = (
            own_sum[1, z_dist, low, :] + far_recv[0, z_dist].astype(F32)
        ).astype(BF16)
        near_send[0, z_dist, high, :] = own_sum[1, z_dist, high, :].astype(BF16)
        near_up[z_dist] = send(near_send.at[0, z_dist], near_recv.at[0, z_dist], x_up)

    def pass_down(z_dist):
        far_copies[z_dist][1].wait_recv()
        near_send[1, z_dist, high, :] = (
            own_sum[3, z_dist, high, :] + far_recv[1, z_dist].astype(F32)
        ).astype(BF16)
        near_send[1, z_dist, low, :] = own_sum[3, z_dist, low, :].astype(BF16)
        near_down[z_dist] = send(near_send.at[1, z_dist], near_recv.at[1, z_dist], x_down)

    for_pair(2)
    for_pair(1)
    for_own(2)
    for d in ORDER:
        far_copies[d] = (send(far_send.at[d, low], far_recv.at[0, d], x_up),
                         send(far_send.at[d, high], far_recv.at[1, d], x_down))
    for_pair(3)
    for_own(1)
    for_pair(0)
    for_own(3)
    for d in ORDER:
        pass_up(d)
        pass_down(d)
    for_own(0)

    line_copies = {}
    for d in ORDER:
        near_up[d].wait_recv()
        near_down[d].wait_recv()
        summed = (
            own_sum[0, d] + near_recv[0, d].astype(F32) + near_recv[1, d].astype(F32)
        )
        if d:
            line_send[d - 1] = summed.astype(BF16)
            line_copies[d] = send(line_send.at[d - 1], line_recv.at[d - 1], line_peers[d])
        else:
            total[...] = summed
    for d in (1, 3, 2):
        line_copies[d].wait_recv()
    average = (
        total[...] + line_recv[0].astype(F32) + line_recv[1].astype(F32) + line_recv[2].astype(F32)
    ) / (Z_LO * X * CORES)
    new_momentum = 0.9 * momentum_ref[...] + average
    out_momentum[...] = new_momentum
    own_rows = pl.ds(pl.multiple_of(rep * share, share), share)
    start_share = w0[own_rows, :].astype(F32)
    out_weights[own_rows, :] = (start_share - 0.7 * (average + 0.9 * new_momentum)).astype(BF16)

    pair_got = []

    def held(d, x_dist, start=0, size=share):
        z_at, x_at = (z_lo + Z_LO - d) % Z_LO, (x + x_dist) % X
        at = ((z_at * X + x_at) * CORES + core) * share + start
        return out_weights.at[pl.ds(pl.multiple_of(at, mid), size), :]

    def keep(d, x_dist):
        here = held(d, x_dist)
        pair_got.append(send(here, here, pair))

    def round_x(d):
        here = held(d, 0)
        return send(here, here, x_up), send(here, here, x_down)

    def onward(d):
        up, down = round_copies[d]
        up.wait_recv()
        here = held(d, X - 1, 0, mid)
        above = send(here, here, x_up)
        down.wait_recv()
        here = held(d, 1, mid, mid)
        below = send(here, here, x_down)
        keep(d, X - 1)
        keep(d, 1)
        return above, below

    own_block = held(0, 0)
    line_got = {d: send(own_block, own_block, line_peers[d]) for d in (1, 3, 2)}
    round_copies = {0: round_x(0)}
    keep(0, 0)
    onward_copies = {}
    for d in (1, 3, 2):
        line_got[d].wait_recv()
        round_copies[d] = round_x(d)
        keep(d, 0)
        previous = {1: 0, 3: 1, 2: 3}[d]
        onward_copies[previous] = onward(previous)
    onward_copies[2] = onward(2)
    for d in (0, 1, 3, 2):
        for copy in onward_copies[d]:
            copy.wait_recv()
        keep(d, 2)

    for copy in pair_got:
        copy.wait_recv()
    for copy in sent:
        copy.wait_send()


def per_device(
    global_weights, momentum, first_moment, second_moment, hidden_bank, target_bank, token_ids
):
    depth, width = global_weights.shape
    block = hidden_bank.shape[1]
    store = target_bank.shape[1]
    inner_count = token_ids.shape[1]
    share = momentum.shape[0]
    anywhere = pl.BlockSpec(memory_space=pl.ANY)
    inside = pl.BlockSpec(memory_space=pltpu.VMEM)
    vmem = pltpu.VMEM
    return pl.pallas_call(
        round_kernel,
        out_shape=(
            vmem((depth, width), BF16),
            vmem((share, width), F32),
        ),
        in_specs=[anywhere, inside, anywhere, anywhere, anywhere, inside, inside],
        out_specs=(inside, inside),
        scratch_shapes=[
            vmem((store, depth), BF16),
            vmem((depth, store), BF16),
            vmem((2, block // 2, depth), BF16),
            vmem((depth, width), BF16),
            vmem((depth, width), F32),
            vmem((depth, width), F32),
            vmem((depth, width), F32),
            vmem((inner_count, store, width), F32),
            vmem((store, width), F32),
            vmem((store, width), BF16),
            vmem((X, Z_LO, share, width), BF16),
            vmem((X, Z_LO, share, width), BF16),
            vmem((X, Z_LO, share, width), F32),
            vmem((Z_LO, share, width), BF16),
            vmem((2, Z_LO, share // 2, width), BF16),
            vmem((2, Z_LO, share, width), BF16),
            vmem((2, Z_LO, share, width), BF16),
            vmem((Z_LO - 1, share, width), BF16),
            vmem((Z_LO - 1, share, width), BF16),
            vmem((share, width), F32),
            pltpu.SemaphoreType.DMA((112,)),
            pltpu.SemaphoreType.DMA((112,)),
            pltpu.SemaphoreType.DMA((4,)),
        ],
        compiler_params=pltpu.CompilerParams(
            collective_id=0, has_side_effects=True, vmem_limit_bytes=60 * 1024 * 1024
        ),
        name="diloco_round",
    )(
        global_weights, momentum, first_moment, second_moment, hidden_bank, target_bank, token_ids
    )


def solution(mesh):
    return jax.shard_map(
        per_device,
        mesh=mesh,
        in_specs=(
            P(None, "fsdp"),
            P("rep", "fsdp"),
            P("rep", None, "fsdp"),
            P("rep", None, "fsdp"),
            P("rep", "fsdp", None),
            P("rep", None, "fsdp"),
            P("rep", None, None),
        ),
        out_specs=(P(None, "fsdp"), P("rep", "fsdp")),
        check_vma=False,
    )
```
